32 devices in a mesh: tok: 2 (over x), voc: 16 (over z, y, core).
Axes of the slice: x: 2, y: 2, z: 4, core: 2. Of those that a mesh axis runs over, the one named last changes fastest.
Arguments:
- hidden: bfloat16 [64, 4608], P(('tok', 'voc')), may hold values from -6 to 6
- norm_gain: float32 [4608], replicated, may hold values from 0.25 to 1.75
- head_weight: bfloat16 [16384, 4608], P(('tok', 'voc')), may hold values from -0.26367188 to 0.26367188
- targets: int32 [64], replicated, may hold values from 0 to 16383
- lengths: int32 [2], replicated, may hold values from 1 to 32
Outputs:
- token_loss: float32 [64], P(('tok', 'voc'))
- mean_loss: float32 [], replicated
The draws below stay inside these ranges and needn't reach their ends.
All inputs are finite; a program needn't handle non-finite values.
Results may differ from the reference program's by a relative error of at most 0.00051.
Values may be sent and summed in bfloat16 or wider, within the bound.
A program may use at most 64 MiB of HBM per device.

```python
import jax
import jax.numpy as jnp
from jax import lax

D = 4608
VOC_DEV = 512
WINDOW = 32
VOCAB = 16384
TOKENS = 64
SEQS = 2


def plant(values, stream_key, least, top_value):
    shape = values.shape
    place = [jax.random.randint(jax.random.fold_in(stream_key, axis), (), 0, shape[axis]) for axis in range(len(shape))]
    values = values.at[tuple(place)].set(least)
    longest = shape.index(max(shape))
    place[longest] = (place[longest] + 1) % shape[longest]
    return values.at[tuple(place)].set(top_value)


def block_scale(rng, shape, shards, low, high):
    level = 1.0
    for dim, parts in shards:
        draws = jax.random.uniform(jax.random.fold_in(jax.random.fold_in(rng, 6), dim), (parts,), jnp.float32, low / len(shards), high / len(shards))
        level = level * jnp.repeat(jnp.exp(draws), shape[dim] // parts).reshape((-1,) + (1,) * (len(shape) - 1 - dim))
    return level


def scatter_about(own_key, dims, width, bound, split=(), held_as=jnp.bfloat16):
    values = jax.random.normal(own_key, dims, jnp.float32) * width
    if len(split) > 0:
        values = block_scale(own_key, dims, split, -0.22, 0.18) * values
    return jnp.clip(values, min=-bound, max=bound).astype(held_as)


def setup_inputs(seed: int = 0) -> dict:
    streams_of = jax.random.split(jax.random.key(seed), 6)
    hidden = scatter_about(streams_of[0], (TOKENS, D), 1.0, 6.0, ((0, 32),))
    norm_gain = jnp.clip(1.0 + 0.15 * jax.random.normal(streams_of[1], (D,), jnp.float32), 0.25, 1.75)
    head_weight = scatter_about(streams_of[2], (VOCAB, D), (3.0 * D ** -0.5), 0.26367188, ((0, 32),))
    targets = plant(jax.random.randint(streams_of[3], (TOKENS,), 0, VOCAB), jax.random.fold_in(streams_of[3], 1), 0, VOCAB - 1).astype(jnp.int32)
    lengths = jax.random.randint(streams_of[4], (SEQS,), 1, WINDOW + 1).astype(jnp.int32)
    return {"hidden": hidden, "norm_gain": norm_gain, "head_weight": head_weight, "targets": targets, "lengths": lengths}


def reference(hidden, norm_gain, head_weight, targets, lengths):
    values = hidden.astype(jnp.float32)
    meansq = lax.optimization_barrier(jnp.mean(values * values, axis=1, keepdims=True))
    normed = (values * lax.rsqrt(meansq + 1e-06) * norm_gain[None, :]).astype(jnp.bfloat16)
    blocks = head_weight.reshape(VOCAB // VOC_DEV, VOC_DEV, D)
    count = VOCAB // VOC_DEV

    def step(carry, item):
        expsum, picked = carry
        block, number = item
        logits = lax.dot_general(normed, block, (((1,), (1,)), ((), ())), preferred_element_type=jnp.float32)
        capped = 30.0 * jnp.tanh(logits / 30.0)
        expsum = expsum + lax.optimization_barrier(jnp.sum(jnp.exp(capped), axis=1))
        local = targets - number * VOC_DEV
        column = jnp.arange(VOC_DEV, dtype=jnp.int32)
        match = column[None, :] == local[:, None]
        picked = picked + lax.optimization_barrier(jnp.sum(jnp.where(match, capped, jnp.zeros_like(capped)), axis=1))
        return ((expsum, picked), None)
    start = (jnp.zeros((TOKENS,), jnp.float32), jnp.zeros((TOKENS,), jnp.float32))
    (expsum, picked), _ = lax.scan(step, start, (blocks, jnp.arange(count, dtype=jnp.int32)))
    position = jnp.arange(WINDOW, dtype=jnp.int32)
    live = (position[None, :] < lengths[:, None]).astype(jnp.float32).reshape(TOKENS)
    token_loss = live * (jnp.log(expsum) - picked)
    mean_loss = jnp.sum(token_loss) / jnp.sum(lengths.astype(jnp.float32))
    return (token_loss, mean_loss)
```

```python
import functools

import jax
import jax.numpy as jnp
from jax import lax
from jax.experimental import pallas as pl
from jax.experimental.pallas import tpu as pltpu
from jax.sharding import PartitionSpec as P

WINDOW = 32
MESH = pl.DeviceIdType.MESH


def kernel(T, H, M, C, seqs, lengths, hidden_hbm, gain_hbm, targets_hbm, head_hbm, tok_out, mean_out,
           hid, gain, targets, head, slots, rows, stats,
           in_sem, head_sem, send_sem, recv_sem, stat_send, stat_recv):
    V = H * M * C
    N = T * V
    own, D = hid.shape
    vocab_rows = head.shape[0]
    pieces = head_sem.shape[0]
    piece = vocab_rows // pieces
    tokens = rows.shape[0]
    G = T * M
    fold = 8 // own
    t = lax.axis_index("tok")
    v = lax.axis_index("voc")
    h, m, c = v // (M * C), (v // C) % M, v % C
    g = t * M + m
    me = t * V + v

    def block(t_, h_, m_, c_):
        return t_ * V + (h_ * M + m_) * C + c_

    def where_a(k):
        return (t, (lax.rem(h + k, H) * M + m) * C + c)

    def where_b(j):
        g_ = lax.rem(g + j, G)
        return (g_ // M, (h * M + g_ % M) * C + c)

    def where_c(i):
        return (t, (h * M + m) * C + lax.rem(c + i, C))

    barrier = pltpu.get_barrier_semaphore()
    for count, where in ((H, where_a), (G, where_b), (C, where_c)):
        def greet(k, _, where=where):
            pl.semaphore_signal(barrier, inc=1, device_id=where(k), device_id_type=MESH)
            return 0
        lax.fori_loop(1, count, greet, 0)

    loads = [
        pltpu.make_async_copy(hidden_hbm, hid, in_sem.at[0]),
        pltpu.make_async_copy(gain_hbm, gain, in_sem.at[1]),
        pltpu.make_async_copy(targets_hbm, targets, in_sem.at[2]),
    ]
    for load in loads:
        load.start()
    heads = [
        pltpu.make_async_copy(head_hbm.at[pl.ds(p * piece, piece)], head.at[pl.ds(p * piece, piece)], head_sem.at[p])
        for p in range(pieces)
    ]
    for load in heads:
        load.start()
    loads[0].wait()
    loads[1].wait()
    values = hid[...].astype(jnp.float32)
    meansq = jnp.mean(values * values, axis=1, keepdims=True)
    normed = (values * lax.rsqrt(meansq + 1e-06) * gain[...]).astype(jnp.bfloat16)
    slots[me] = normed
    pl.semaphore_wait(barrier, (H - 1) + (G - 1) + (C - 1))

    def copy(b, number, device):
        return pltpu.make_async_remote_copy(
            src_ref=slots.at[b], dst_ref=slots.at[b], send_sem=send_sem.at[number], recv_sem=recv_sem.at[b],
            device_id=device, device_id_type=MESH)

    def arrived(b):
        copy(b, 0, where_a(1)).wait_recv()

    def merge(b):
        eight = pl.ds(pl.multiple_of(b // fold * 8, 8), 8)
        mine = lax.broadcasted_iota(jnp.int32, (8, 1), 0) // own == b % fold
        rows[eight, :] = jnp.where(mine, jnp.concatenate([slots[b].astype(jnp.float32)] * fold, axis=0), rows[eight, :])

    first_b = H - 1
    first_c = first_b + H * (G - 1)

    def send_a(k, _):
        copy(me, k - 1, where_a(k)).start()
        return 0

    def pass_b(k, b):
        def one(j, _):
            copy(b, first_b + k * (G - 1) + j - 1, where_b(j)).start()
            return 0
        lax.fori_loop(1, G, one, 0)

    def pass_c(n, b):
        def one(i, _):
            copy(b, first_c + n * (C - 1) + i - 1, where_c(i)).start()
            return 0
        lax.fori_loop(1, C, one, 0)

    lax.fori_loop(1, H, send_a, 0)
    pass_b(0, me)
    pass_c(0, me)
    merge(me)

    def take_a(k, _):
        b = block(t, lax.rem(h + k, H), m, c)
        arrived(b)
        pass_b(k, b)
        pass_c(k, b)
        merge(b)
        return 0
    lax.fori_loop(1, H, take_a, 0)

    def take_b(n, _):
        k, j = n // (G - 1), n % (G - 1) + 1
        g_ = lax.rem(g + j, G)
        b = block(g_ // M, lax.rem(h + k, H), g_ % M, c)
        arrived(b)
        pass_c(H + n, b)
        merge(b)
        return 0
    lax.fori_loop(0, H * (G - 1), take_b, 0)

    def take_c(n, _):
        i, r = n // (G * H) + 1, n % (G * H)
        k, g_ = r // G, lax.rem(g + r % G, G)
        b = block(g_ // M, lax.rem(h + k, H), g_ % M, lax.rem(c + i, C))
        arrived(b)
        merge(b)
        return 0
    lax.fori_loop(0, (C - 1) * G * H, take_c, 0)

    for load in heads:
        load.wait()
    logits = lax.dot_general(
        head[...], rows[...].astype(jnp.bfloat16), (((1,), (1,)), ((), ())), preferred_element_type=jnp.float32)
    capped = 30.0 * jnp.tanh(logits / 30.0)
    expsum = jnp.sum(jnp.exp(capped), axis=0, keepdims=True)
    loads[2].wait()
    wanted = targets[...] - me * vocab_rows
    column = lax.broadcasted_iota(jnp.int32, capped.shape, 0)
    picked = jnp.sum(jnp.where(column == wanted, capped, 0.0), axis=0, keepdims=True)
    stats[me] = jnp.concatenate([expsum, picked], axis=0)

    def stat_copy(b, k, device):
        return pltpu.make_async_remote_copy(
            src_ref=stats.at[b], dst_ref=stats.at[b], send_sem=stat_send.at[k], recv_sem=stat_recv.at[b],
            device_id=device, device_id_type=MESH)

    def stat_start(k, _):
        d = lax.rem(me + k, N)
        stat_copy(me, k - 1, (d // V, d % V)).start()
        return 0
    lax.fori_loop(1, N, stat_start, 0)

    def sent(k, _):
        copy(me, k, where_a(1)).wait_send()
        return 0
    lax.fori_loop(0, N - 1, sent, 0)

    lane = lax.broadcasted_iota(jnp.int32, (1, tokens), 1)
    live = jnp.zeros((1, tokens), jnp.float32)
    total = jnp.int32(0)
    for s in range(seqs):
        position = lane - s * WINDOW
        size = lengths[s]
        total = total + size
        live = live + jnp.where((position >= 0) & (position < size) & (position < WINDOW), 1.0, 0.0)

    def stat_take(k, _):
        stat_copy(lax.rem(me + k, N), k - 1, where_a(1)).wait_recv()
        return 0
    lax.fori_loop(1, N, stat_take, 0)
    def stat_sent(k, _):
        stat_copy(me, k - 1, where_a(1)).wait_send()
        return 0
    lax.fori_loop(1, N, stat_sent, 0)
    totals = jnp.sum(stats[...], axis=0)
    loss = live * (jnp.log(totals[0:1]) - totals[1:2])
    count = jnp.full((1, 1), total, jnp.int32).astype(jnp.float32)
    mean_out[...] = jnp.sum(loss, axis=1, keepdims=True) / count
    tok_out[...] = jnp.concatenate(
        [jnp.sum(jnp.where(lane == me * own + r, loss, 0.0), axis=1, keepdims=True) for r in range(own)], axis=1)


def solution(mesh):
    T, V = mesh.shape["tok"], mesh.shape["voc"]
    C = 2 if V % 2 == 0 else 1
    M = 2 if (V // C) % 2 == 0 else 1
    H = V // (C * M)
    N = T * V

    def body(hidden, norm_gain, head_weight, targets, lengths):
        own, D = hidden.shape
        vocab_rows = head_weight.shape[0]
        tokens = own * N
        pieces = 4 if vocab_rows % 64 == 0 else 1
        hbm = pl.BlockSpec(memory_space=pl.ANY)
        token_loss, mean_loss = pl.pallas_call(
            functools.partial(kernel, T, H, M, C, lengths.shape[0]),
            out_shape=(jax.ShapeDtypeStruct((1, own), jnp.float32), jax.ShapeDtypeStruct((1, 1), jnp.float32)),
            in_specs=[pl.BlockSpec(memory_space=pltpu.SMEM), hbm, hbm, hbm, hbm],
            out_specs=(pl.BlockSpec(memory_space=pltpu.VMEM), pl.BlockSpec(memory_space=pltpu.VMEM)),
            scratch_shapes=[
                pltpu.VMEM((own, D), jnp.bfloat16),
                pltpu.VMEM((1, D), jnp.float32),
                pltpu.VMEM((1, tokens), jnp.int32),
                pltpu.VMEM((vocab_rows, D), jnp.bfloat16),
                pltpu.VMEM((N, own, D), jnp.bfloat16),
                pltpu.VMEM((tokens, D), jnp.float32),
                pltpu.VMEM((N, 2, tokens), jnp.float32),
                pltpu.SemaphoreType.DMA((3,)),
                pltpu.SemaphoreType.DMA((pieces,)),
                pltpu.SemaphoreType.DMA((N - 1,)),
                pltpu.SemaphoreType.DMA((N,)),
                pltpu.SemaphoreType.DMA((N - 1,)),
                pltpu.SemaphoreType.DMA((N,)),
            ],
            compiler_params=pltpu.CompilerParams(
                collective_id=0, has_side_effects=True, vmem_limit_bytes=60 * 1024 * 1024),
        )(lengths, hidden, norm_gain.reshape(1, D), targets.reshape(1, tokens), head_weight)
        return token_loss.reshape(own), mean_loss.reshape(())

    in_specs = (P(("tok", "voc"), None), P(), P(("tok", "voc"), None), P(), P())
    out_specs = (P(("tok", "voc")), P())
    return jax.shard_map(body, mesh=mesh, in_specs=in_specs, out_specs=out_specs, check_vma=False)
```

```python
import functools

import jax
import jax.numpy as jnp
from jax import lax
from jax.experimental import pallas as pl
from jax.experimental.pallas import tpu as pltpu
from jax.sharding import PartitionSpec as P

WINDOW = 32
MESH = pl.DeviceIdType.MESH


def loop(low, high, step):
    if high - low <= 32:
        for k in range(low, high):
            step(k, 0)
    else:
        lax.fori_loop(low, high, step, 0)


def kernel(T, H, M, C, seqs, lengths, hidden_hbm, gain_hbm, targets_hbm, head_hbm, tok_out, mean_out,
           hid, gain, targets, head, slots, stats,
           in_sem, head_sem, send_sem, recv_sem, stat_send, stat_recv):
    V = H * M * C
    N = T * V
    own, D = hid.shape
    vocab_rows = head.shape[0]
    pieces = head_sem.shape[0]
    piece = vocab_rows // pieces
    tokens = N * own
    G = T * M
    t = lax.axis_index("tok")
    v = lax.axis_index("voc")
    h, m, c = v // (M * C), (v // C) % M, v % C
    g = t * M + m
    me = t * V + v

    def block(t_, h_, m_, c_):
        return t_ * V + (h_ * M + m_) * C + c_

    def where_a(k):
        return (t, (lax.rem(h + k, H) * M + m) * C + c)

    def where_b(j):
        g_ = lax.rem(g + j, G)
        return (g_ // M, (h * M + g_ % M) * C + c)

    def where_c(i):
        return (t, (h * M + m) * C + lax.rem(c + i, C))

    barrier = pltpu.get_barrier_semaphore()
    for count, where in ((H, where_a), (G, where_b), (C, where_c)):
        def greet(k, _, where=where):
            pl.semaphore_signal(barrier, inc=1, device_id=where(k), device_id_type=MESH)
            return 0
        loop(1, count, greet)

    loads = [
        pltpu.make_async_copy(hidden_hbm, hid, in_sem.at[0]),
        pltpu.make_async_copy(gain_hbm, gain, in_sem.at[1]),
        pltpu.make_async_copy(targets_hbm, targets, in_sem.at[2]),
    ]
    for load in loads:
        load.start()
    heads = [
        pltpu.make_async_copy(head_hbm.at[pl.ds(p * piece, piece)], head.at[pl.ds(p * piece, piece)], head_sem.at[p])
        for p in range(pieces)
    ]
    for load in heads:
        load.start()
    loads[0].wait()
    loads[1].wait()
    values = hid[...].astype(jnp.float32)
    meansq = jnp.mean(values * values, axis=1, keepdims=True)
    normed = (values * lax.rsqrt(meansq + 1e-06) * gain[...].reshape(1, D)).astype(jnp.bfloat16)
    slots[me] = normed
    pl.semaphore_wait(barrier, (H - 1) + (G - 1) + (C - 1))

    def copy(b, sem, device):
        return pltpu.make_async_remote_copy(
            src_ref=slots.at[b], dst_ref=slots.at[b], send_sem=send_sem.at[0], recv_sem=recv_sem.at[sem],
            device_id=device, device_id_type=MESH)

    def blocks(first, number, sem):
        part = slots.at[pl.ds(first, number)]
        return pltpu.make_async_remote_copy(
            src_ref=part, dst_ref=part, send_sem=send_sem.at[0], recv_sem=recv_sem.at[sem],
            device_id=where_a(1), device_id_type=MESH)

    def arrived(b):
        copy(b, b, where_a(1)).wait_recv()

    def send_a(k, _):
        copy(me, me, where_a(k)).start()
        return 0

    def pass_b(b):
        def one(j, _):
            copy(b, b, where_b(j)).start()
            return 0
        loop(1, G, one)

    def pass_c(b):
        def one(i, _):
            copy(b, N, where_c(i)).start()
            return 0
        loop(1, C, one)

    loop(1, H, send_a)
    pass_b(me)
    pass_c(me)

    def take_a(k, _):
        b = block(t, lax.rem(h + k, H), m, c)
        arrived(b)
        pass_b(b)
        pass_c(b)
        return 0
    loop(1, H, take_a)

    def take_b(n, _):
        k, j = n // (G - 1), n % (G - 1) + 1
        g_ = lax.rem(g + j, G)
        b = block(g_ // M, lax.rem(h + k, H), g_ % M, c)
        arrived(b)
        pass_c(b)
        return 0
    loop(0, H * (G - 1), take_b)

    if C > 1:
        blocks(0, (C - 1) * G * H, N).wait_recv()

    for load in heads:
        load.wait()
    logits = lax.dot_general(
        head[...], slots[...].reshape(tokens, D), (((1,), (1,)), ((), ())), preferred_element_type=jnp.float32)
    capped = 30.0 * jnp.tanh(logits / 30.0)
    expsum = jnp.sum(jnp.exp(capped), axis=0, keepdims=True)
    loads[2].wait()
    wanted = targets[...] - me * vocab_rows
    column = lax.broadcasted_iota(jnp.int32, capped.shape, 0)
    picked = jnp.sum(jnp.where(column == wanted, capped, 0.0), axis=0, keepdims=True)
    stats[me] = jnp.concatenate([expsum, picked], axis=0)

    def stat_copy(b, k, device):
        return pltpu.make_async_remote_copy(
            src_ref=stats.at[b], dst_ref=stats.at[b], send_sem=stat_send.at[0], recv_sem=stat_recv.at[0],
            device_id=device, device_id_type=MESH)

    def stat_start(k, _):
        d = lax.rem(me + k, N)
        stat_copy(me, k - 1, (d // V, d % V)).start()
        return 0
    loop(1, N, stat_start)

    blocks(0, N - 1, 0).wait_send()

    lane = lax.broadcasted_iota(jnp.int32, (1, tokens), 1)
    live = jnp.zeros((1, tokens), jnp.float32)
    total = jnp.int32(0)
    for s in range(seqs):
        position = lane - s * WINDOW
        size = lengths[s]
        total = total + size
        live = live + jnp.where((position >= 0) & (position < size) & (position < WINDOW), 1.0, 0.0)

    everyone = pltpu.make_async_remote_copy(
        src_ref=stats.at[pl.ds(0, N - 1)], dst_ref=stats.at[pl.ds(0, N - 1)], send_sem=stat_send.at[0],
        recv_sem=stat_recv.at[0], device_id=where_a(1), device_id_type=MESH)
    everyone.wait_send()
    everyone.wait_recv()
    totals = jnp.sum(stats[...], axis=0)
    loss = live * (jnp.log(totals[0:1]) - totals[1:2])
    mean_out[0] = jnp.sum(loss) / total.astype(jnp.float32)
    for r in range(own):
        tok_out[r] = jnp.sum(jnp.where(lane == me * own + r, loss, 0.0))


def solution(mesh):
    T, V = mesh.shape["tok"], mesh.shape["voc"]
    C = 2 if V % 2 == 0 else 1
    M = 2 if (V // C) % 2 == 0 else 1
    H = V // (C * M)
    N = T * V

    def body(hidden, norm_gain, head_weight, targets, lengths):
        own, D = hidden.shape
        vocab_rows = head_weight.shape[0]
        tokens = own * N
        pieces = 4 if vocab_rows % 64 == 0 else 1
        hbm = pl.BlockSpec(memory_space=pl.ANY)
        token_loss, mean_loss = pl.pallas_call(
            functools.partial(kernel, T, H, M, C, lengths.shape[0]),
            out_shape=(jax.ShapeDtypeStruct((own,), jnp.float32), jax.ShapeDtypeStruct((1,), jnp.float32)),
            in_specs=[pl.BlockSpec(memory_space=pltpu.SMEM), hbm, hbm, hbm, hbm],
            out_specs=(pl.BlockSpec(memory_space=pltpu.SMEM), pl.BlockSpec(memory_space=pltpu.SMEM)),
            scratch_shapes=[
                pltpu.VMEM((own, D), jnp.bfloat16),
                pltpu.VMEM((D,), jnp.float32),
                pltpu.VMEM((1, tokens), jnp.int32),
                pltpu.VMEM((vocab_rows, D), jnp.bfloat16),
                pltpu.VMEM((N, own, D), jnp.bfloat16),
                pltpu.VMEM((N, 2, tokens), jnp.float32),
                pltpu.SemaphoreType.DMA((3,)),
                pltpu.SemaphoreType.DMA((pieces,)),
                pltpu.SemaphoreType.DMA((1,)),
                pltpu.SemaphoreType.DMA((N + 1,)),
                pltpu.SemaphoreType.DMA((1,)),
                pltpu.SemaphoreType.DMA((1,)),
            ],
            compiler_params=pltpu.CompilerParams(
                collective_id=0, has_side_effects=True, vmem_limit_bytes=60 * 1024 * 1024),
        )(lengths, hidden, norm_gain, targets.reshape(1, tokens), head_weight)
        return token_loss, mean_loss.reshape(())

    in_specs = (P(("tok", "voc"), None), P(), P(("tok", "voc"), None), P(), P())
    out_specs = (P(("tok", "voc")), P())
    return jax.shard_map(body, mesh=mesh, in_specs=in_specs, out_specs=out_specs, check_vma=False)
```

```python
import functools

import jax
import jax.numpy as jnp
from jax import lax
from jax.experimental import pallas as pl
from jax.experimental.pallas import tpu as pltpu
from jax.sharding import PartitionSpec as P

WINDOW = 32
MESH = pl.DeviceIdType.MESH


def loop(low, high, step):
    if high - low <= 32:
        for k in range(low, high):
            step(k, 0)
    else:
        lax.fori_loop(low, high, step, 0)


def other(mine, k, size):
    if size & (size - 1) == 0:
        return mine ^ k
    return lax.rem(mine + k, size)


def kernel(T, H, M, C, seqs, lengths, hidden_hbm, gain_hbm, targets_hbm, head_hbm, tok_out, mean_out,
           hid, gain, targets, head, slots, stats,
           in_sem, head_sem, send_sem, recv_sem, stat_send, stat_recv):
    V = H * M * C
    N = T * V
    own, D = hid.shape
    vocab_rows = head.shape[0]
    pieces = head_sem.shape[0]
    piece = vocab_rows // pieces
    tokens = N * own
    G = T * M
    t = lax.axis_index("tok")
    v = lax.axis_index("voc")
    h, m, c = v // (M * C), (v // C) % M, v % C
    g = t * M + m
    me = t * V + v

    def block(t_, h_, m_, c_):
        return t_ * V + (h_ * M + m_) * C + c_

    def where_a(k):
        return (t, (other(h, k, H) * M + m) * C + c)

    def where_b(j):
        g_ = other(g, j, G)
        return (g_ // M, (h * M + g_ % M) * C + c)

    def where_c(i):
        return (t, (h * M + m) * C + other(c, i, C))

    loads = [
        pltpu.make_async_copy(hidden_hbm, hid, in_sem.at[0]),
        pltpu.make_async_copy(gain_hbm, gain, in_sem.at[1]),
        pltpu.make_async_copy(targets_hbm, targets, in_sem.at[2]),
    ]
    for load in loads:
        load.start()
    barrier = pltpu.get_barrier_semaphore()
    for count, where in ((H, where_a), (G, where_b), (C, where_c)):
        def greet(k, _, where=where):
            pl.semaphore_signal(barrier, inc=1, device_id=where(k), device_id_type=MESH)
            return 0
        loop(1, count, greet)

    loads[0].wait()
    loads[1].wait()
    values = hid[...].astype(jnp.float32)
    meansq = jnp.mean(values * values, axis=1, keepdims=True)
    normed = (values * lax.rsqrt(meansq + 1e-06) * gain[...].reshape(1, D)).astype(jnp.bfloat16)
    slots[me] = normed
    pl.semaphore_wait(barrier, (H - 1) + (G - 1) + (C - 1))

    def copy(b, sem, device):
        return pltpu.make_async_remote_copy(
            src_ref=slots.at[b], dst_ref=slots.at[b], send_sem=send_sem.at[0], recv_sem=recv_sem.at[sem],
            device_id=device, device_id_type=MESH)

    def blocks(first, number, sem):
        part = slots.at[pl.ds(first, number)]
        return pltpu.make_async_remote_copy(
            src_ref=part, dst_ref=part, send_sem=send_sem.at[0], recv_sem=recv_sem.at[sem],
            device_id=where_a(1), device_id_type=MESH)

    def arrived(b):
        copy(b, b, where_a(1)).wait_recv()

    def send_a(k, _):
        copy(me, me, where_a(H - k)).start()
        return 0

    def pass_b(b):
        def one(j, _):
            copy(b, b, where_b(G - j)).start()
            return 0
        loop(1, G, one)

    def pass_c(b):
        def one(i, _):
            copy(b, N, where_c(i)).start()
            return 0
        loop(1, C, one)

    loop(1, H, send_a)
    pass_b(me)
    pass_c(me)

    heads = [
        pltpu.make_async_copy(head_hbm.at[pl.ds(p * piece, piece)], head.at[pl.ds(p * piece, piece)], head_sem.at[p])
        for p in range(pieces)
    ]
    for load in heads:
        load.start()

    def take_a(k, _):
        b = block(t, other(h, k, H), m, c)
        arrived(b)
        pass_b(b)
        pass_c(b)
        return 0
    loop(1, H, take_a)

    def take_b(n, _):
        k, j = n // (G - 1), n % (G - 1) + 1
        g_ = other(g, j, G)
        b = block(g_ // M, other(h, k, H), g_ % M, c)
        arrived(b)
        pass_c(b)
        return 0
    loop(0, H * (G - 1), take_b)

    if C > 1:
        blocks(0, (C - 1) * G * H, N).wait_recv()

    for load in heads:
        load.wait()
    logits = lax.dot_general(
        head[...], slots[...].reshape(tokens, D), (((1,), (1,)), ((), ())), preferred_element_type=jnp.float32)
    capped = 30.0 * jnp.tanh(logits / 30.0)
    expsum = jnp.sum(jnp.exp(capped), axis=0, keepdims=True)
    loads[2].wait()
    wanted = targets[...] - me * vocab_rows
    column = lax.broadcasted_iota(jnp.int32, capped.shape, 0)
    picked = jnp.sum(jnp.where(column == wanted, capped, 0.0), axis=0, keepdims=True)
    stats[me] = jnp.concatenate([expsum, picked], axis=0)

    def stat_copy(b, k, device):
        return pltpu.make_async_remote_copy(
            src_ref=stats.at[b], dst_ref=stats.at[b], send_sem=stat_send.at[0], recv_sem=stat_recv.at[0],
            device_id=device, device_id_type=MESH)

    def stat_start(k, _):
        d = other(me, N - k, N)
        stat_copy(me, k - 1, (d // V, d % V)).start()
        return 0
    loop(1, N, stat_start)

    blocks(0, N - 1, 0).wait_send()

    lane = lax.broadcasted_iota(jnp.int32, (1, tokens), 1)
    live = jnp.zeros((1, tokens), jnp.float32)
    total = jnp.int32(0)
    for s in range(seqs):
        position = lane - s * WINDOW
        size = lengths[s]
        total = total + size
        live = live + jnp.where((position >= 0) & (position < size) & (position < WINDOW), 1.0, 0.0)

    everyone = pltpu.make_async_remote_copy(
        src_ref=stats.at[pl.ds(0, N - 1)], dst_ref=stats.at[pl.ds(0, N - 1)], send_sem=stat_send.at[0],
        recv_sem=stat_recv.at[0], device_id=where_a(1), device_id_type=MESH)
    everyone.wait_send()
    everyone.wait_recv()
    totals = jnp.sum(stats[...], axis=0)
    loss = live * (jnp.log(totals[0:1]) - totals[1:2])
    mean_out[0] = jnp.sum(loss) / total.astype(jnp.float32)
    for r in range(own):
        tok_out[r] = jnp.sum(jnp.where(lane == me * own + r, loss, 0.0))


def solution(mesh):
    T, V = mesh.shape["tok"], mesh.shape["voc"]
    C = 2 if V % 2 == 0 else 1
    M = 2 if (V // C) % 2 == 0 else 1
    H = V // (C * M)
    N = T * V

    def body(hidden, norm_gain, head_weight, targets, lengths):
        own, D = hidden.shape
        vocab_rows = head_weight.shape[0]
        tokens = own * N
        pieces = 4 if vocab_rows % 64 == 0 else 1
        hbm = pl.BlockSpec(memory_space=pl.ANY)
        token_loss, mean_loss = pl.pallas_call(
            functools.partial(kernel, T, H, M, C, lengths.shape[0]),
            out_shape=(jax.ShapeDtypeStruct((own,), jnp.float32), jax.ShapeDtypeStruct((1,), jnp.float32)),
            in_specs=[pl.BlockSpec(memory_space=pltpu.SMEM), hbm, hbm, hbm, hbm],
            out_specs=(pl.BlockSpec(memory_space=pltpu.SMEM), pl.BlockSpec(memory_space=pltpu.SMEM)),
            scratch_shapes=[
                pltpu.VMEM((own, D), jnp.bfloat16),
                pltpu.VMEM((D,), jnp.float32),
                pltpu.VMEM((1, tokens), jnp.int32),
                pltpu.VMEM((vocab_rows, D), jnp.bfloat16),
                pltpu.VMEM((N, own, D), jnp.bfloat16),
                pltpu.VMEM((N, 2, tokens), jnp.float32),
                pltpu.SemaphoreType.DMA((3,)),
                pltpu.SemaphoreType.DMA((pieces,)),
                pltpu.SemaphoreType.DMA((1,)),
                pltpu.SemaphoreType.DMA((N + 1,)),
                pltpu.SemaphoreType.DMA((1,)),
                pltpu.SemaphoreType.DMA((1,)),
            ],
            compiler_params=pltpu.CompilerParams(
                collective_id=0, has_side_effects=True, vmem_limit_bytes=60 * 1024 * 1024),
        )(lengths, hidden, norm_gain, targets.reshape(1, tokens), head_weight)
        return token_loss, mean_loss.reshape(())

    in_specs = (P(("tok", "voc"), None), P(), P(("tok", "voc"), None), P(), P())
    out_specs = (P(("tok", "voc")), P())
    return jax.shard_map(body, mesh=mesh, in_specs=in_specs, out_specs=out_specs, check_vma=False)
```

```python
import functools

import jax
import jax.numpy as jnp
from jax import lax
from jax.experimental import pallas as pl
from jax.experimental.pallas import tpu as pltpu
from jax.sharding import PartitionSpec as P

WINDOW = 32
MESH = pl.DeviceIdType.MESH


def loop(low, high, step):
    if high - low <= 32:
        for k in range(low, high):
            step(k, 0)
    else:
        lax.fori_loop(low, high, step, 0)


def other(mine, k, size):
    if size & (size - 1) == 0:
        return mine ^ k
    return lax.rem(mine + k, size)


def kernel(T, H, M, C, seqs, lengths, hidden_hbm, gain_hbm, targets_hbm, head_hbm, tok_out, mean_out,
           hid, gain, targets, head, slots, stats,
           in_sem, head_sem, send_sem, recv_sem, stat_send, stat_recv):
    V = H * M * C
    N = T * V
    own, D = hid.shape
    vocab_rows = head.shape[0]
    pieces = head_sem.shape[0]
    piece = vocab_rows // pieces
    tokens = N * own
    G = T * M
    t = lax.axis_index("tok")
    v = lax.axis_index("voc")
    h, m, c = v // (M * C), (v // C) % M, v % C
    g = t * M + m
    me = t * V + v

    def block(t_, h_, m_, c_):
        return t_ * V + (h_ * M + m_) * C + c_

    def where_a(k):
        return (t, (other(h, k, H) * M + m) * C + c)

    def where_b(j):
        g_ = other(g, j, G)
        return (g_ // M, (h * M + g_ % M) * C + c)

    def where_c(i):
        return (t, (h * M + m) * C + other(c, i, C))

    loads = [
        pltpu.make_async_copy(hidden_hbm, hid, in_sem.at[0]),
        pltpu.make_async_copy(gain_hbm, gain, in_sem.at[1]),
        pltpu.make_async_copy(targets_hbm, targets, in_sem.at[2]),
    ]
    for load in loads:
        load.start()
    barrier = pltpu.get_barrier_semaphore()
    for count, where in ((H, where_a), (G, where_b), (C, where_c)):
        def greet(k, _, where=where):
            pl.semaphore_signal(barrier, inc=1, device_id=where(k), device_id_type=MESH)
            return 0
        loop(1, count, greet)

    loads[0].wait()
    loads[1].wait()
    values = hid[...].astype(jnp.float32)
    meansq = jnp.mean(values * values, axis=1, keepdims=True)
    normed = (values * lax.rsqrt(meansq + 1e-06) * gain[...].reshape(1, D)).astype(jnp.bfloat16)
    slots[me] = normed
    pl.semaphore_wait(barrier, (H - 1) + (G - 1) + (C - 1))

    def copy(b, sem, device):
        return pltpu.make_async_remote_copy(
            src_ref=slots.at[b], dst_ref=slots.at[b], send_sem=send_sem.at[0], recv_sem=recv_sem.at[sem],
            device_id=device, device_id_type=MESH)

    def blocks(first, number, sem):
        part = slots.at[pl.ds(first, number)]
        return pltpu.make_async_remote_copy(
            src_ref=part, dst_ref=part, send_sem=send_sem.at[0], recv_sem=recv_sem.at[sem],
            device_id=where_a(1), device_id_type=MESH)

    def arrived(b):
        copy(b, b, where_a(1)).wait_recv()

    def send_a(k, _):
        copy(me, me, where_a(H - k)).start()
        return 0

    def pass_b(b):
        def one(j, _):
            copy(b, b, where_b(G - j)).start()
            return 0
        loop(1, G, one)

    def pass_c(b):
        def one(i, _):
            copy(b, N, where_c(i)).start()
            return 0
        loop(1, C, one)

    loop(1, H, send_a)
    pass_b(me)
    pass_c(me)

    heads = [
        pltpu.make_async_copy(head_hbm.at[pl.ds(p * piece, piece)], head.at[pl.ds(p * piece, piece)], head_sem.at[p])
        for p in range(pieces)
    ]
    for load in heads:
        load.start()

    def take_a(k, _):
        b = block(t, other(h, k, H), m, c)
        arrived(b)
        pass_b(b)
        pass_c(b)
        return 0
    loop(1, H, take_a)

    def take_b(n, _):
        k, j = n // (G - 1), n % (G - 1) + 1
        g_ = other(g, j, G)
        b = block(g_ // M, other(h, k, H), g_ % M, c)
        arrived(b)
        pass_c(b)
        return 0
    loop(0, H * (G - 1), take_b)

    if C > 1:
        blocks(0, (C - 1) * G * H, N).wait_recv()

    for load in heads:
        load.wait()
    logits = lax.dot_general(
        head[...], slots[...].reshape(tokens, D), (((1,), (1,)), ((), ())), preferred_element_type=jnp.float32)
    capped = 30.0 * jnp.tanh(logits / 30.0)
    expsum = jnp.sum(jnp.exp(capped), axis=0, keepdims=True)
    loads[2].wait()
    wanted = targets[...] - me * vocab_rows
    column = lax.broadcasted_iota(jnp.int32, capped.shape, 0)
    picked = jnp.sum(jnp.where(column == wanted, capped, 0.0), axis=0, keepdims=True)
    stats[me] = jnp.concatenate([expsum, picked], axis=1)

    def stat_copy(b, k, device):
        return pltpu.make_async_remote_copy(
            src_ref=stats.at[b], dst_ref=stats.at[b], send_sem=stat_send.at[0], recv_sem=stat_recv.at[0],
            device_id=device, device_id_type=MESH)

    def stat_start(k, _):
        d = other(me, N - k, N)
        stat_copy(me, k - 1, (d // V, d % V)).start()
        return 0
    loop(1, N, stat_start)

    blocks(0, N - 1, 0).wait_send()

    lane = lax.broadcasted_iota(jnp.int32, (1, tokens), 1)
    live = jnp.zeros((1, tokens), jnp.float32)
    total = jnp.int32(0)
    for s in range(seqs):
        position = lane - s * WINDOW
        size = lengths[s]
        total = total + size
        live = live + jnp.where((position >= 0) & (position < size) & (position < WINDOW), 1.0, 0.0)

    everyone = pltpu.make_async_remote_copy(
        src_ref=stats.at[pl.ds(0, N - 1)], dst_ref=stats.at[pl.ds(0, N - 1)], send_sem=stat_send.at[0],
        recv_sem=stat_recv.at[0], device_id=where_a(1), device_id_type=MESH)
    everyone.wait_send()
    everyone.wait_recv()
    totals = jnp.sum(stats[...], axis=0)
    loss = live * (jnp.log(totals[:, :tokens]) - totals[:, tokens:])
    mean_out[0] = jnp.sum(loss) / total.astype(jnp.float32)
    for r in range(own):
        tok_out[r] = jnp.sum(jnp.where(lane == me * own + r, loss, 0.0))


def solution(mesh):
    T, V = mesh.shape["tok"], mesh.shape["voc"]
    C = 2 if V % 2 == 0 else 1
    M = 2 if (V // C) % 2 == 0 else 1
    H = V // (C * M)
    N = T * V

    def body(hidden, norm_gain, head_weight, targets, lengths):
        own, D = hidden.shape
        vocab_rows = head_weight.shape[0]
        tokens = own * N
        pieces = 4 if vocab_rows % 64 == 0 else 1
        hbm = pl.BlockSpec(memory_space=pl.ANY)
        token_loss, mean_loss = pl.pallas_call(
            functools.partial(kernel, T, H, M, C, lengths.shape[0]),
            out_shape=(jax.ShapeDtypeStruct((own,), jnp.float32), jax.ShapeDtypeStruct((1,), jnp.float32)),
            in_specs=[pl.BlockSpec(memory_space=pltpu.SMEM), hbm, hbm, hbm, hbm],
            out_specs=(pl.BlockSpec(memory_space=pltpu.SMEM), pl.BlockSpec(memory_space=pltpu.SMEM)),
            scratch_shapes=[
                pltpu.VMEM((own, D), jnp.bfloat16),
                pltpu.VMEM((D,), jnp.float32),
                pltpu.VMEM((1, tokens), jnp.int32),
                pltpu.VMEM((vocab_rows, D), jnp.bfloat16),
                pltpu.VMEM((N, own, D), jnp.bfloat16),
                pltpu.VMEM((N, 1, 2 * tokens), jnp.float32),
                pltpu.SemaphoreType.DMA((3,)),
                pltpu.SemaphoreType.DMA((pieces,)),
                pltpu.SemaphoreType.DMA((1,)),
                pltpu.SemaphoreType.DMA((N + 1,)),
                pltpu.SemaphoreType.DMA((1,)),
                pltpu.SemaphoreType.DMA((1,)),
            ],
            compiler_params=pltpu.CompilerParams(
                collective_id=0, has_side_effects=True, vmem_limit_bytes=60 * 1024 * 1024),
        )(lengths, hidden, norm_gain, targets.reshape(1, tokens), head_weight)
        return token_loss, mean_loss.reshape(())

    in_specs = (P(("tok", "voc"), None), P(), P(("tok", "voc"), None), P(), P())
    out_specs = (P(("tok", "voc")), P())
    return jax.shard_map(body, mesh=mesh, in_specs=in_specs, out_specs=out_specs, check_vma=False)
```
